32 devices in a mesh: groups: 2 (over x), wide: 16 (over z, y, core).
Axes of the slice: x: 2, y: 2, z: 4, core: 2. Of those that a mesh axis runs over, the one named last changes fastest.
Arguments:
- queries: bfloat16 [4096, 4096], P(('groups', 'wide')), parts along dimension 0, may hold values from -64 to 64
- first_keys: bfloat16 [4096, 4096], P(('groups', 'wide')), parts along dimension 0, may hold values from -4 to 4
- first_values: bfloat16 [4096, 4096], P(('groups', 'wide')), parts along dimension 0, may hold values from -6 to 6
- second_keys: bfloat16 [4096, 4096], P(('groups', 'wide')), parts along dimension 0, may hold values from -4 to 4
- second_values: bfloat16 [4096, 4096], P(('groups', 'wide')), parts along dimension 0, may hold values from -6 to 6
- out_weight: bfloat16 [4096, 2048], P('wide'), may hold values from -0.09375 to 0.09375
- norm_gain: float32 [2048], replicated, may hold values from 0.1 to 1.9
- gate_weight: bfloat16 [32, 2048, 768], P('wide'), may hold values from -0.125 to 0.125
- up_weight: bfloat16 [32, 2048, 768], P('wide'), may hold values from -0.125 to 0.125
- down_weight: bfloat16 [32, 768, 2048], P('wide'), may hold values from -0.21875 to 0.21875
- routes: int32 [4096, 4], P(('groups', 'wide')), parts along dimension 0, may hold values from 0 to 255, as said below
- route_weights: float32 [4096, 4], P(('groups', 'wide')), parts along dimension 0, may hold values from 0.2 to 1
Outputs:
- layer_out: bfloat16 [4096, 2048], P(('groups', 'wide')), parts along dimension 0
The draws below stay inside these ranges and needn't reach their ends.
There are 2 independent parts, one for each index of `groups`. The reference program is written for one: setup_inputs(seed, part) draws one part's arguments, and reference() takes and returns one part's arrays. A program takes and returns all parts, laid end to end along the dimension named above; an argument that names none is the same for every part. Nothing has to cross between parts.
Inputs may be any that keep to these rules, and one draw needn't show every extreme that they name: `routes`: each token names four different experts. Every expert is named by exactly 32 tokens of the sequence, and by at most 4 tokens among the rows of one device; each expert is named exactly 4 times by the rows of some device.
All inputs are finite; a program needn't handle non-finite values.
Results may differ from the reference program's by a relative error of at most 0.03.
Values may be sent and summed in bfloat16 or wider, within the bound.
No kernel may reach another device: no remote copies, remote signals or barrier semaphores. Data moves between devices by JAX's collectives and lax.ppermute only.
A program may use at most 192 MiB of HBM per device.

```python
import math
import jax
import jax.numpy as jnp
from jax import lax

TOK_DEV = 128
HEADS = 32
HEAD_DIM = 128
WIN_KEYS = 512
WIN_PAIRS = 12
D = 2048
FF = 768
EXPERTS = 256
FLIGHT_DEV = 2
SEQ = 2048
FLIGHT = 32
N_WIDE = 16


def simplex_fields(key):
    field_shape = (SEQ, HEADS, HEAD_DIM)
    query_field = 3.0 * jax.random.truncated_normal(jax.random.fold_in(key, 101), -6.0, 6.0, field_shape)
    first_field = jax.random.truncated_normal(jax.random.fold_in(key, 102), -4.0, 4.0, field_shape)
    second_field = jax.random.truncated_normal(jax.random.fold_in(key, 103), -4.0, 4.0, field_shape)
    flat_shape = (SEQ, HEADS * HEAD_DIM)
    return (query_field.reshape(flat_shape), first_field.reshape(flat_shape), second_field.reshape(flat_shape))


def draw_queries(key, part):
    return simplex_fields(key)[0].astype(jnp.bfloat16)


def draw_first_keys(key, part):
    return simplex_fields(key)[1].astype(jnp.bfloat16)


def draw_second_keys(key, part):
    return simplex_fields(key)[2].astype(jnp.bfloat16)


def draw_routes(key, part):
    pair_count = SEQ // (2 * TOK_DEV)
    subkeys = jax.random.split(jax.random.fold_in(key, 201), pair_count)
    orders = jax.vmap(lambda subkey: jax.random.permutation(subkey, EXPERTS))(subkeys)
    halves = orders.reshape(2 * pair_count, EXPERTS // 2)
    columns = jnp.arange(4 * TOK_DEV) % (EXPERTS // 2)
    return halves[:, columns].reshape(SEQ, 4).astype(jnp.int32)


def steps_of(rng, dims, cuts, least, high):
    def one(dim, blocks):
        steps = jax.random.uniform(jax.random.fold_in(jax.random.fold_in(rng, 6), dim), (blocks,), jnp.float32, least / len(cuts), high / len(cuts))
        return jnp.repeat(jnp.exp(steps), dims[dim] // blocks).reshape((-1,) + (1,) * (len(dims) - dim - 1))

    level = one(*cuts[0])
    for cut in cuts[1:]:
        level = level * one(*cut)
    return level


def centred(own_key, extent, width, reach, cuts=(), held_as=jnp.bfloat16):
    level = steps_of(own_key, extent, cuts, -0.22, 0.18) if cuts else 1.0
    values = jax.random.normal(own_key, extent, jnp.float32) * width * level
    return jnp.minimum(jnp.maximum(values, -reach), reach).astype(held_as)


def setup_inputs(seed: int = 0, part: int = 0) -> dict:
    seeds = jax.random.split(jax.random.key(seed), 13)
    part_keys = jax.random.split(jax.random.fold_in(seeds[12], part), 13)
    queries = draw_queries(jax.random.fold_in(jax.random.fold_in(seeds[12], part), 71), part)
    first_keys = draw_first_keys(jax.random.fold_in(jax.random.fold_in(seeds[12], part), 71), part)
    first_values = centred(part_keys[2], (SEQ, HEADS * HEAD_DIM), 1.0, 6.0, ((0, 16),))
    second_keys = draw_second_keys(jax.random.fold_in(jax.random.fold_in(seeds[12], part), 71), part)
    second_values = centred(part_keys[4], (SEQ, HEADS * HEAD_DIM), 1.0, 6.0, ((0, 16),))
    out_weight = centred(seeds[5], (HEADS * HEAD_DIM, D), (HEADS * HEAD_DIM) ** -0.5, 0.09375, ((0, 16),))
    norm_gain = jnp.clip(1.0 + 0.18 * jax.random.normal(seeds[6], (D,), jnp.float32), 0.1, 1.9)
    gate_weight = centred(seeds[7], (FLIGHT, D, FF), D ** -0.5, 0.125, ((0, 16),))
    up_weight = centred(seeds[8], (FLIGHT, D, FF), D ** -0.5, 0.125, ((0, 16),))
    down_weight = centred(seeds[9], (FLIGHT, FF, D), FF ** -0.5, 0.21875, ((0, 16),))
    routes = draw_routes(jax.random.fold_in(jax.random.fold_in(seeds[12], part), 71), part)
    route_weights = jnp.clip(0.2 + 0.8 * jax.random.uniform(part_keys[11], (SEQ, 4), jnp.float32) ** steps_of(part_keys[11], (SEQ, 4), ((0, 16),), -0.2, 0.2), 0.2, 1.0)
    return dict(queries=queries, first_keys=first_keys, first_values=first_values, second_keys=second_keys, second_values=second_values, out_weight=out_weight, norm_gain=norm_gain, gate_weight=gate_weight, up_weight=up_weight, down_weight=down_weight, routes=routes, route_weights=route_weights)


def window_stack(extended, length):
    return jnp.stack([extended[WIN_PAIRS - 1 - offset:WIN_PAIRS - 1 - offset + length] for offset in range(WIN_PAIRS)], axis=1)

def group_attention(pieces, query_start, key_start):
    query_rows, keys_window, values_window, pair_keys_ext, pair_values_ext = pieces
    length = query_rows.shape[0]
    pair_keys = window_stack(pair_keys_ext, length)
    pair_values = window_stack(pair_values_ext, length)
    pair_query = (query_rows[:, None].astype(jnp.float32) * pair_keys.astype(jnp.float32)).astype(jnp.bfloat16)
    scores = jnp.einsum('trgd,lgd->tgrl', pair_query.astype(jnp.float32), keys_window.astype(jnp.float32)) * (1.0 / math.sqrt(HEAD_DIM))
    query_pos = query_start + jnp.arange(length, dtype=jnp.int32)
    key_pos = key_start + jnp.arange(keys_window.shape[0], dtype=jnp.int32)
    offsets = jnp.arange(WIN_PAIRS, dtype=jnp.int32)
    near_mask = (key_pos[None, :] <= query_pos[:, None]) & (key_pos[None, :] > query_pos[:, None] - WIN_KEYS) & (key_pos[None, :] >= 0)
    pair_mask = query_pos[:, None] - offsets[None, :] >= 0
    allowed = near_mask[:, None, None, :] & pair_mask[:, None, :, None]
    scores = jnp.where(allowed, scores, -jnp.inf)
    row_top = lax.optimization_barrier(jnp.max(scores, axis=(2, 3), keepdims=True))
    raised = jnp.exp(scores - row_top)
    weights = (raised / lax.optimization_barrier(jnp.sum(raised, axis=(2, 3), keepdims=True))).astype(jnp.bfloat16)
    partial_value = jnp.einsum('tgrl,lgd->tgrd', weights.astype(jnp.float32), values_window.astype(jnp.float32))
    combined = lax.optimization_barrier(jnp.sum(partial_value * pair_values.transpose(0, 2, 1, 3).astype(jnp.float32), axis=2))
    return combined.astype(jnp.bfloat16)

def reference(queries, first_keys, first_values, second_keys, second_values, out_weight, norm_gain, gate_weight, up_weight, down_weight, routes, route_weights):
    length = TOK_DEV
    reach_blocks = (WIN_KEYS + length - 2) // length
    feature_width = HEADS * HEAD_DIM
    per_step = math.gcd(HEADS, 4)
    groups = HEADS // per_step
    far_zeros = jnp.zeros((reach_blocks * length, feature_width), jnp.bfloat16)
    near_zeros = jnp.zeros((WIN_PAIRS - 1, feature_width), jnp.bfloat16)
    keys_padded = jnp.concatenate([far_zeros, first_keys], axis=0)
    values_padded = jnp.concatenate([far_zeros, first_values], axis=0)
    pair_keys_padded = jnp.concatenate([near_zeros, second_keys], axis=0)
    pair_values_padded = jnp.concatenate([near_zeros, second_values], axis=0)

    def split_heads(matrix):
        return matrix.reshape(matrix.shape[0], groups, per_step, HEAD_DIM).transpose(1, 0, 2, 3)

    def one_block(block_index):
        start_row = block_index * length
        window_rows = (reach_blocks + 1) * length
        pieces = (split_heads(lax.dynamic_slice_in_dim(queries, start_row, length, 0)), split_heads(lax.dynamic_slice_in_dim(keys_padded, start_row, window_rows, 0)), split_heads(lax.dynamic_slice_in_dim(values_padded, start_row, window_rows, 0)), split_heads(lax.dynamic_slice_in_dim(pair_keys_padded, start_row, length + WIN_PAIRS - 1, 0)), split_heads(lax.dynamic_slice_in_dim(pair_values_padded, start_row, length + WIN_PAIRS - 1, 0)))
        key_start = start_row - reach_blocks * length
        result = lax.map(lambda group_pieces: group_attention(group_pieces, start_row, key_start), pieces)
        return result.transpose(1, 0, 2, 3).reshape(length, feature_width)
    attended = lax.map(one_block, jnp.arange(N_WIDE, dtype=jnp.int32)).reshape(SEQ, feature_width)
    projected = jnp.dot(attended, out_weight, preferred_element_type=jnp.float32).astype(jnp.bfloat16)
    wide_proj = projected.astype(jnp.float32)
    normed = (wide_proj * lax.rsqrt(lax.optimization_barrier(jnp.mean(wide_proj * wide_proj, axis=1, keepdims=True)) + 1e-06) * norm_gain).astype(jnp.bfloat16)
    expert_load = 4 * SEQ // EXPERTS

    def expert_step(accum, expert):
        hit_mask = routes == expert
        member = jnp.any(hit_mask, axis=1)
        token_index = jnp.nonzero(member, size=expert_load)[0]
        rows_in = normed[token_index]
        gate_proj = jnp.dot(rows_in, gate_weight[expert], preferred_element_type=jnp.float32)
        upward = jnp.dot(rows_in, up_weight[expert], preferred_element_type=jnp.float32)
        hidden = (jax.nn.silu(gate_proj) * upward).astype(jnp.bfloat16)
        result = jnp.dot(hidden, down_weight[expert], preferred_element_type=jnp.float32).astype(jnp.bfloat16)
        route_scale = lax.optimization_barrier(jnp.sum(jnp.where(hit_mask, route_weights, jnp.float32(0.0)), axis=1))[token_index]
        return (accum.at[token_index].add(route_scale[:, None] * result.astype(jnp.float32)), None)
    expert_sum, unused = lax.scan(expert_step, jnp.zeros((SEQ, D), jnp.float32), jnp.arange(FLIGHT_DEV * N_WIDE, dtype=jnp.int32))
    return (wide_proj + expert_sum).astype(jnp.bfloat16)
```

```python
import functools
import math

import jax
import jax.numpy as jnp
from jax import lax
from jax.experimental import pallas as pl
from jax.experimental.pallas import tpu as pltpu
from jax.sharding import PartitionSpec as P

HEAD_DIM = 128
WIN_KEYS = 512
WIN_PAIRS = 12
HALO = 16
CAP = 4


def attention_body(rows_step, place, q_own, k_own, v_own, k2_own, v2_own, partner, near, far, halo,
                   out_ref, keys, values, seconds, second_values, scores, tops):
    core, chip = place[0], place[1]
    length = q_own.shape[0]
    first = core == 0
    f32, bf16 = jnp.float32, jnp.bfloat16

    def in_order(mine, other):
        return jnp.where(first, mine, other), jnp.where(first, other, mine)

    q = in_order(q_own[...], partner[0])
    k = in_order(k_own[...], partner[1])
    v = in_order(v_own[...], partner[2])
    k2 = in_order(k2_own[...], partner[3])
    v2 = in_order(v2_own[...], partner[4])
    near_k, near_v = in_order(near[0], near[1]), in_order(near[2], near[3])
    far_k, far_v = in_order(far[0], far[1]), in_order(far[2], far[3])
    start_key = jnp.where(chip == 0, k[0][0:1], near_k[0][0:1])
    fill = jnp.broadcast_to(start_key, k[0].shape)
    for a in range(2):
        at = lambda block: slice(block * length, (block + 1) * length)
        keys[at(a)] = jnp.where(chip >= 2, far_k[a], fill)
        keys[at(2 + a)] = jnp.where(chip >= 1, near_k[a], fill)
        keys[at(4 + a)] = k[a]
        nothing = jnp.zeros_like(v[a])
        one = jnp.ones_like(v[a])
        values[at(a), :HEAD_DIM] = jnp.where(chip >= 2, far_v[a], nothing)
        values[at(a), HEAD_DIM:] = jnp.where(chip >= 2, one, nothing)
        values[at(2 + a), :HEAD_DIM] = jnp.where(chip >= 1, near_v[a], nothing)
        values[at(2 + a), HEAD_DIM:] = jnp.where(chip >= 1, one, nothing)
        values[at(4 + a), :HEAD_DIM] = v[a]
        values[at(4 + a), HEAD_DIM:] = one
        second = k2[a].astype(f32)
        seconds[a, HALO:] = second
        second_values[a, HALO:, :HEAD_DIM] = v2[a].astype(f32)
        second_values[a, HALO:, HEAD_DIM:] = jnp.ones((length, HEAD_DIM), f32)
        if a == 0:
            seconds[a, :HALO] = jnp.where(
                chip == 0, jnp.broadcast_to(second[0:1], (HALO, HEAD_DIM)), halo[0].astype(f32))
            there = jnp.where(chip == 0, 0.0, 1.0).astype(f32)
            second_values[a, :HALO, :HEAD_DIM] = jnp.where(
                chip == 0, jnp.zeros((HALO, HEAD_DIM), f32), halo[1].astype(f32))
            second_values[a, :HALO, HEAD_DIM:] = jnp.broadcast_to(there, (HALO, HEAD_DIM))
        else:
            seconds[a, :HALO] = k2[0][length - HALO:].astype(f32)
            second_values[a, :HALO, :HEAD_DIM] = v2[0][length - HALO:].astype(f32)
            second_values[a, :HALO, HEAD_DIM:] = jnp.ones((HALO, HEAD_DIM), f32)

    scale = math.log2(math.e) / math.sqrt(HEAD_DIM)
    span = 5 * length
    steps = [(a, row) for a in range(2) for row in range(0, length, rows_step)]

    def causal(row):
        t = lax.broadcasted_iota(jnp.int32, (rows_step, length), 0) + row
        return lax.broadcasted_iota(jnp.int32, (rows_step, length), 1) <= t

    def score(slot, a, row):
        scaled = q[a][row:row + rows_step].astype(f32) * scale
        pair_query = jnp.concatenate(
            [(scaled * seconds[a, HALO - r + row:HALO - r + row + rows_step]).astype(bf16)
             for r in range(WIN_PAIRS)], axis=0)
        raw = lax.dot_general(pair_query, keys[a * length:a * length + span], (((1,), (1,)), ((), ())),
                              preferred_element_type=f32).reshape(WIN_PAIRS, rows_step, span)
        edge = jnp.where(causal(row)[None], raw[:, :, 4 * length:], raw[:, :, :length])
        top = jnp.max(edge, axis=0)
        scores[slot, :, :, :length] = edge
        for block in range(1, 4):
            part = raw[:, :, block * length:(block + 1) * length]
            scores[slot, :, :, block * length:(block + 1) * length] = part
            top = jnp.maximum(top, jnp.max(part, axis=0))
        tops[slot] = jnp.broadcast_to(jnp.max(top, axis=1, keepdims=True), top.shape)

    def gather(slot, a, row):
        top = tops[slot][None]
        part = [jnp.exp2(scores[slot, :, :, block * length:(block + 1) * length] - top).astype(bf16)
                for block in range(4)]
        mask = causal(row)[None]
        empty = jnp.zeros_like(part[0])
        weights = jnp.concatenate(
            [jnp.where(mask, empty, part[0]), *part[1:], jnp.where(mask, part[0], empty)], axis=2)
        summed = jnp.dot(weights.reshape(WIN_PAIRS * rows_step, span), values[a * length:a * length + span],
                         preferred_element_type=f32).reshape(WIN_PAIRS, rows_step, 2 * HEAD_DIM)
        total = summed[0] * second_values[a, HALO + row:HALO + row + rows_step]
        for r in range(1, WIN_PAIRS):
            total += summed[r] * second_values[a, HALO - r + row:HALO - r + row + rows_step]
        out = total[:, :HEAD_DIM] / total[:, HEAD_DIM:]
        out_ref[a ^ core, row:row + rows_step] = out.astype(bf16)

    score(0, *steps[0])
    for i, step in enumerate(steps):
        if i + 1 < len(steps):
            score((i + 1) % 2, *steps[i + 1])
        gather(i % 2, *step)


def attention(place, own, partner, near, far, halo, head0, run, rows_step=64):
    length = own[0].shape[0]
    heads = near.shape[2] // HEAD_DIM

    def column(h, place):
        head = head0 + h
        return (0, (head // run) * 2 * run + place[0] * run + head % run)

    own_spec = pl.BlockSpec((length, HEAD_DIM), column)
    lead = lambda n, rows, off: pl.BlockSpec((n, rows, HEAD_DIM), lambda h, place: (0, 0, off + h))
    return pl.pallas_call(
        functools.partial(attention_body, rows_step),
        out_shape=jax.ShapeDtypeStruct((2, length, heads * HEAD_DIM), jnp.bfloat16),
        grid_spec=pltpu.PrefetchScalarGridSpec(
            num_scalar_prefetch=1, grid=(heads,),
            in_specs=[own_spec] * 5 + [lead(5, length, head0), lead(4, length, 0), lead(4, length, 0),
                                       lead(2, HALO, head0)],
            out_specs=lead(2, length, 0),
            scratch_shapes=[
                pltpu.VMEM((6 * length, HEAD_DIM), jnp.bfloat16),
                pltpu.VMEM((6 * length, 2 * HEAD_DIM), jnp.bfloat16),
                pltpu.VMEM((2, HALO + length, HEAD_DIM), jnp.float32),
                pltpu.VMEM((2, HALO + length, 2 * HEAD_DIM), jnp.float32),
                pltpu.VMEM((2, WIN_PAIRS, rows_step, WIN_KEYS), jnp.float32),
                pltpu.VMEM((2, rows_step, HEAD_DIM), jnp.float32),
            ]),
        compiler_params=pltpu.CompilerParams(dimension_semantics=("arbitrary",), vmem_limit_bytes=48 << 20),
        cost_estimate=pl.CostEstimate(
            flops=heads * 2 * 2 * 2 * WIN_PAIRS * length * 5 * length * HEAD_DIM,
            bytes_accessed=heads * 24 * length * HEAD_DIM * 2, transcendentals=0),
    )(place, *own, partner, near, far, halo)


def half_columns(x, run, core):
    length, width = x.shape
    parts = x.reshape(length, width // (2 * run), 2, run)
    return lax.dynamic_index_in_dim(parts, core, 2, keepdims=False).reshape(length, width // 2)


def on_device(
    queries,
    first_keys,
    first_values,
    second_keys,
    second_values,
    out_weight,
    norm_gain,
    gate_weight,
    up_weight,
    down_weight,
    routes,
    route_weights,
):
    length, feature_width = queries.shape
    device = lax.axis_index("wide")
    devices = lax.axis_size("wide")
    core, chip = device % 2, device // 2
    weight_rows = out_weight.shape[0]
    run = weight_rows // HEAD_DIM
    swap = [(i, i ^ 1) for i in range(devices)]

    def chips_on(x, by):
        return lax.ppermute(x, "wide", [(i, i + 2 * by) for i in range(devices - 2 * by)])

    full_weight = lax.all_gather(out_weight, "wide", axis=0, tiled=True)
    model_width = out_weight.shape[1]
    own = (queries, first_keys, first_values, second_keys, second_values)
    partner = lax.ppermute(
        jnp.stack([half_columns(x, weight_rows, 1 - core) for x in own]), "wide", swap)
    mine = [half_columns(x, weight_rows, core) for x in own[1:]]
    message = jnp.stack([mine[0], partner[1], mine[1], partner[2]])
    tails = jnp.where(
        core == 1,
        jnp.stack([x[length - HALO :] for x in mine[2:]]),
        partner[3:, length - HALO :],
    )
    halo = chips_on(tails, 1)
    near = chips_on(message, 1)
    far = chips_on(message, 2)
    place = jnp.stack([core, chip]).astype(jnp.int32)
    attended = attention(place, own, partner, near, far, halo, 0, run)
    own_rows = lax.dynamic_index_in_dim(
        full_weight.reshape(devices // 2, 2, weight_rows, model_width), core, 1, keepdims=False
    ).reshape(feature_width // 2, model_width)
    partial = jnp.dot(
        attended.reshape(2 * length, feature_width // 2), own_rows,
        preferred_element_type=jnp.float32,
    ).reshape(2, length, model_width)
    projected32 = partial[0] + lax.ppermute(partial[1], "wide", swap)
    projected = projected32.astype(jnp.bfloat16)
    wide_proj = projected.astype(jnp.float32)
    normed = (
        wide_proj
        * lax.rsqrt(jnp.mean(wide_proj * wide_proj, axis=1, keepdims=True) + 1e-06)
        * norm_gain
    ).astype(jnp.bfloat16)
    local_experts = gate_weight.shape[0]
    flight = local_experts * devices
    slot_count = flight * CAP
    route_count = routes.shape[1]
    flat_routes = routes.reshape(-1)
    expert_hits = (flat_routes[:, None] == jnp.arange(flight, dtype=jnp.int32)[None, :]).astype(
        jnp.int32
    )
    earlier = jnp.cumsum(expert_hits, axis=0) - expert_hits
    ranking = jnp.sum(earlier * expert_hits, axis=1)
    in_flight = flat_routes < flight
    target = jnp.where(in_flight, flat_routes * CAP + ranking, slot_count)
    chooser = target[None, :] == jnp.arange(slot_count, dtype=jnp.int32)[:, None]
    token_chooser = jnp.any(chooser.reshape(slot_count, length, route_count), axis=2)
    outgoing = jnp.dot(
        token_chooser.astype(jnp.bfloat16), normed, preferred_element_type=jnp.float32
    ).astype(jnp.bfloat16)
    outgoing = outgoing.reshape(devices, local_experts, CAP, model_width)
    arrived = lax.all_to_all(outgoing, "wide", split_axis=0, concat_axis=0, tiled=True)
    sources, experts_here, kept_slots, row_width = arrived.shape
    expert_rows = arrived.transpose(1, 0, 2, 3).reshape(
        experts_here, sources * kept_slots, row_width
    )
    gate_proj = jnp.einsum(
        "erd,edf->erf", expert_rows, gate_weight, preferred_element_type=jnp.float32
    )
    upward = jnp.einsum("erd,edf->erf", expert_rows, up_weight, preferred_element_type=jnp.float32)
    hidden = (jax.nn.silu(gate_proj) * upward).astype(jnp.bfloat16)
    result = jnp.einsum(
        "erf,efd->erd", hidden, down_weight, preferred_element_type=jnp.float32
    ).astype(jnp.bfloat16)
    finished = result.reshape(experts_here, sources, kept_slots, row_width).transpose(1, 0, 2, 3)
    returned = lax.all_to_all(finished, "wide", split_axis=0, concat_axis=0, tiled=True).reshape(
        slot_count, model_width
    )
    picked = jnp.take(returned, jnp.minimum(target, slot_count - 1), axis=0).astype(jnp.float32)
    route_scale = jnp.where(in_flight, route_weights.reshape(-1), jnp.float32(0.0))
    expert_sum = jnp.sum(
        (picked * route_scale[:, None]).reshape(length, route_count, model_width), axis=1
    )
    return (wide_proj + expert_sum).astype(jnp.bfloat16)


def solution(mesh):
    in_specs = (
        P(("groups", "wide"), None),
        P(("groups", "wide"), None),
        P(("groups", "wide"), None),
        P(("groups", "wide"), None),
        P(("groups", "wide"), None),
        P("wide", None),
        P(),
        P("wide", None, None),
        P("wide", None, None),
        P("wide", None, None),
        P(("groups", "wide"), None),
        P(("groups", "wide"), None),
    )
    out_specs = P(("groups", "wide"), None)
    return jax.shard_map(
        on_device, mesh=mesh, in_specs=in_specs, out_specs=out_specs, check_vma=False
    )
```
